512 devices in a mesh: blk: 128 (over z, y, core), tok: 4 (over x).
Axes of the slice: x: 4, y: 8, z: 8, core: 2. Of those that a mesh axis runs over, the one named last changes fastest.
Arguments:
- queries: bfloat16 [4096, 32, 128], P('blk'), may hold values from -0.5 to 0.5
- candidates: int32 [4096, 4], P('blk'), may hold values from 0 to 127, all different within a row; in each aligned block of 32 rows (0 to 31, 32 to 63, ...) at most 2 rows name the same one
- passages: bfloat16 [128, 180, 32, 128], P('blk', 'tok'), may hold values from -0.5 to 0.5
- lengths: int32 [128, 32], P('blk'), may hold values from 1 to 180
Outputs:
- maxsim: float32 [4096, 4, 32], P('blk', None, 'tok')
The draws below stay inside these ranges and needn't reach their ends.
Inputs may be any that keep to these rules, and one draw needn't show every extreme that they name: `candidates`: each row names 4 different blocks. Among the rows of one index of blk no block is named more than 2 times, and in every draw some block is named exactly 2 times by the rows of some index.
All inputs are finite; a program needn't handle non-finite values.
Results may differ from the reference program's by a relative error of at most 0.0003.
Values may be sent and summed in bfloat16 or wider, within the bound.
No kernel may reach another device: no remote copies, remote signals or barrier semaphores. Data moves between devices by JAX's collectives and lax.ppermute only.
A program may use at most 64 MiB of HBM per device.

```python
import math
import jax
import jax.numpy as jnp
import numpy as np
from jax import lax

DIM = 128
QT = 32
PT = 180
PASS = 32
QDEV = 32
K = 4
BLOCKS = 128
QUERIES = 4096
CAP = 2


def with_ends(drawn, rng, smallest, top_value):
    extent = drawn.shape
    spot = [jax.random.randint(jax.random.fold_in(rng, axis), (), 0, extent[axis]) for axis in range(len(extent))]
    drawn = drawn.at[tuple(spot)].set(smallest)
    longest = extent.index(max(extent))
    spot[longest] = (spot[longest] + 1) % extent[longest]
    return drawn.at[tuple(spot)].set(top_value)


def block_scale(stream_key, extent, split, low, top_value):
    def one(axis_at, parts):
        draws = jax.random.uniform(jax.random.fold_in(jax.random.fold_in(stream_key, 6), axis_at), (parts,), jnp.float32, low / len(split), top_value / len(split))
        return jnp.repeat(jnp.exp(draws), extent[axis_at] // parts).reshape((-1,) + (1,) * (len(extent) - axis_at - 1))

    loudness = one(*split[0])
    for cut in split[1:]:
        loudness = loudness * one(*cut)
    return loudness


def deal_out(key, own, number, rows, count, top, limit, slope):
    ranking = jax.random.permutation(key, count)
    crowded, ordinary = load_shares(count, rows * top, limit, slope, True), load_shares(count, rows * top, limit, slope, False)
    places = jnp.arange(count)

    def named(sizes, turn):
        used = int((sizes > 0).sum())
        fixed = max(1, used // 4)
        shifted = fixed + (places - fixed + turn * (used - fixed)) % max(1, count - fixed)
        return jnp.zeros((count,), jnp.int32).at[ranking[jnp.where(places < fixed, places, shifted)]].set(jnp.asarray(sizes, jnp.int32))

    sizes = jnp.where(number % 4 == 0, named(crowded, number // 4), named(ordinary, number - number // 4 - 1))
    mixed = jax.random.permutation(jax.random.fold_in(own, 3), count)
    source_of, receiver = mixed[0:count // 2 * 2:2], mixed[1:count // 2 * 2:2]
    room = jnp.minimum(sizes[source_of] - 1, limit - sizes[receiver]) // 2
    room = jnp.where((source_of == ranking[0]) | (receiver == ranking[0]) | (sizes[receiver] == 0), 0, jnp.maximum(room, 0))
    shifted = jax.random.randint(jax.random.fold_in(own, 4), (count // 2,), 0, 1 << 20) % (room + 1)
    sizes = sizes.at[source_of].add(-shifted).at[receiver].add(shifted)
    members = jnp.searchsorted(jnp.cumsum(sizes), jnp.arange(rows * top), side="right").astype(jnp.int32)
    listing = members.reshape(top, rows).T
    listing = listing[jax.random.permutation(jax.random.fold_in(own, 1), rows)]
    turn = jax.random.randint(jax.random.fold_in(own, 2), (rows, 1), 0, top)
    return jnp.take_along_axis(listing, (jnp.arange(top)[None, :] + turn) % top, axis=1)


def load_shares(count, total, reach, lean, full):
    weights = [(1 << 20) // math.isqrt(rank ** lean) + 1 for rank in range(1, count + 1)]
    largest = reach if full else min(reach, max(-(-total // count), total * weights[0] // sum(weights)))
    least = 1 if total - largest >= count - 1 else 0
    given, spare = [largest] + [least] * (count - 1), total - largest - least * (count - 1)
    while spare > 0:
        movable = [i for i in range(1, count) if given[i] < largest] or [i for i in range(1, count) if given[i] < reach]
        mass, remaining = sum([weights[i] for i in movable]), spare
        for i in movable:
            extra = min(reach - given[i], max(1, remaining * weights[i] // mass), spare)
            given[i] = given[i] + extra
            spare = spare - extra
    return np.array(given)


def bell_draw(key, dims, width, bound, cuts=(), kind=jnp.bfloat16):
    result = jax.random.normal(key, dims, jnp.float32) * width
    if len(cuts) > 0:
        result = block_scale(key, dims, cuts, -0.22, 0.18) * result
    return jnp.clip(result, min=-bound, max=bound).astype(kind)


def setup_inputs(seed: int = 0) -> dict:
    arg_keys = jax.random.split(jax.random.key(seed), 5)
    queries = bell_draw(arg_keys[0], (QUERIES, QT, DIM), DIM ** -0.5, 0.5, ((0, 128),))
    candidates_keys = jax.random.split(jax.random.fold_in(arg_keys[1], 1), QUERIES // QDEV)
    candidates_turns = jax.random.permutation(jax.random.fold_in(arg_keys[1], 3), QUERIES // QDEV)
    candidates = jax.vmap(lambda own, number: deal_out(jax.random.fold_in(arg_keys[1], 2), own, number, QDEV, BLOCKS, K, CAP, 2))(candidates_keys, candidates_turns).reshape((QUERIES, K))
    passages = bell_draw(arg_keys[2], (BLOCKS, PT, PASS, DIM), DIM ** -0.5, 0.5, ((0, 128), (1, 4)))
    lengths = with_ends(jax.random.randint(arg_keys[3], (BLOCKS, PASS), 1, PT + 1), jax.random.fold_in(arg_keys[3], 1), 1, PT).astype(jnp.int32)
    return dict(queries=queries, candidates=candidates, passages=passages, lengths=lengths)


NEGATIVE_FILL = -1.0e30


def reference(queries, candidates, passages, lengths):
    token_pos = jnp.arange(passages.shape[1], dtype=jnp.int32)

    def one_query(packed):
        query_tile, cand_row = packed
        query_wide = query_tile.astype(jnp.float32)

        def one_block(block_id):
            passage = passages[block_id].astype(jnp.float32)
            valid_mask = token_pos[:, None] < lengths[block_id][None, :]
            scores = jnp.einsum("qd,tpd->qtp", query_wide, passage)
            scores = jnp.where(valid_mask[None], scores, NEGATIVE_FILL)
            return jnp.sum(jnp.max(scores, axis=1), axis=0)

        return jax.vmap(one_block)(cand_row)

    return lax.map(one_query, (queries, candidates))
```

```python
import itertools

import jax
import jax.numpy as jnp
from jax import lax
from jax.experimental import pallas as pl
from jax.experimental.pallas import tpu as pltpu
from jax.sharding import PartitionSpec as P


CORES = 2
VMEM = pl.BlockSpec(memory_space=pltpu.VMEM)
SMEM = pl.BlockSpec(memory_space=pltpu.SMEM)


def build_kernel(cand_ref, query_ref, out_ref, table):
    pair_k, pair_q = cand_ref.shape
    owners = table.shape[0]
    core = lax.axis_index("blk") % CORES
    plane = lax.axis_index("tok")
    owner_core = core ^ (plane // 2)
    backward = plane % 2 == 0
    pairs = pair_k * pair_q
    for d in range(owners):
        table[d] = 0
    for i in range(pairs):
        p = jnp.where(backward, pairs - 1 - i, i)
        table[cand_ref[p // pair_q, p % pair_q]] = p % pair_q
    for d in range(owners // CORES):
        out_ref[d] = query_ref[table[d * CORES + owner_core]]


def score_kernel(pass_ref, query_ref, out_ref, *, tile, piece, query_len):
    slots_len, width, dim = pass_ref.shape
    items = tile // query_len

    def one_tile(index, carry):
        rows = query_ref[pl.ds(pl.multiple_of(index * tile, tile), tile), :]
        best = None
        for start in range(0, slots_len, piece):
            segment = pass_ref[start : start + piece].reshape(piece * width, dim)
            scores = lax.dot_general(
                segment, rows, (((1,), (1,)), ((), ())), preferred_element_type=jnp.float32
            )
            top = jnp.max(scores.reshape(piece, width, tile), axis=0)
            best = top if best is None else jnp.maximum(best, top)
        flipped = jnp.transpose(best).reshape(items, query_len, width)
        out_ref[pl.ds(pl.multiple_of(index * items, items), items), :] = jnp.sum(flipped, axis=1)
        return carry

    lax.fori_loop(0, query_ref.shape[0] // tile, one_tile, 0)


def turn_kernel(in_ref, out_ref):
    parts, cores, part_width, slots = out_ref.shape
    flipped = jnp.transpose(in_ref[...])
    for part in range(parts):
        for core in range(cores):
            out_ref[part, core] = flipped[part * part_width : (part + 1) * part_width]


def pick_kernel(in_ref, lane_ref, plane_ref, out_ref):
    planes, cores, part_width, slots = in_ref.shape
    cand_count, _, query_count = out_ref.shape
    lanes = jnp.broadcast_to(lane_ref[...], (part_width, cores * slots))
    which = jnp.broadcast_to(plane_ref[...], (part_width, cores * slots))
    picked = None
    for plane in range(planes):
        row = jnp.concatenate([in_ref[plane, core] for core in range(cores)], axis=1)
        got = jnp.take_along_axis(row, lanes, axis=1)
        picked = got if picked is None else jnp.where(which == plane, got, picked)
    for k in range(cand_count):
        out_ref[k] = picked[:, k * query_count : (k + 1) * query_count]


def make_groups(mesh):
    owners = mesh.shape["blk"]
    parts = mesh.shape["tok"]
    chips = owners // CORES
    same_core = [[chip * CORES + core for chip in range(chips)] for core in range(CORES)]
    around = [
        [(chip * CORES + core) * parts + part for part in range(parts) for core in range(CORES)]
        for chip in range(chips)
    ]
    swap = []
    for blk, part in itertools.product(range(owners), range(parts)):
        source = blk * parts + part
        swap.append((source, source if part < parts // 2 else (blk ^ 1) * parts + part))
    return same_core, around, swap


def shards(queries, candidates, passages, lengths, *, same_core, around, swap):
    num_owners = lax.axis_size("blk")
    num_parts = lax.axis_size("tok")
    part_idx = lax.axis_index("tok")
    core = lax.axis_index("blk") % CORES
    query_count, query_len, dim_width = queries.shape
    cand_count = candidates.shape[1]
    local_len = passages.shape[1]
    pass_width = passages.shape[2]
    part_width = pass_width // num_parts
    chips = num_owners // CORES

    turned = candidates.T
    outgoing = pl.pallas_call(
        build_kernel,
        out_shape=jax.ShapeDtypeStruct((chips, query_len, dim_width), queries.dtype),
        in_specs=[SMEM, VMEM],
        out_specs=VMEM,
        scratch_shapes=[pltpu.SMEM((num_owners,), jnp.int32)],
        name="build",
    )(turned, queries)
    outgoing = lax.ppermute(outgoing, ("blk", "tok"), swap)
    received = lax.all_to_all(
        outgoing, "blk", split_axis=0, concat_axis=0, axis_index_groups=same_core, tiled=True
    )

    own = passages[0]
    pieces = [own] + [
        lax.ppermute(own, "tok", [(i, (i + shift) % num_parts) for i in range(num_parts)])
        for shift in range(1, num_parts)
    ]
    stacked = jnp.stack(pieces)
    origin = (part_idx - jnp.arange(num_parts, dtype=jnp.int32)) % num_parts
    token_pos = origin[:, None] * local_len + jnp.arange(local_len, dtype=jnp.int32)[None, :]
    valid = token_pos[:, :, None] < lengths[0][None, None, :]
    first = lax.dynamic_index_in_dim(stacked[:, 0], part_idx, 0, keepdims=False)
    tokens = jnp.where(valid[..., None], stacked, first[None, None])
    tokens = tokens.reshape(num_parts * local_len, pass_width, dim_width)

    totals = pl.pallas_call(
        lambda *refs: score_kernel(*refs, tile=512, piece=60, query_len=query_len),
        out_shape=jax.ShapeDtypeStruct((chips, pass_width), jnp.float32),
        in_specs=[VMEM, VMEM],
        out_specs=VMEM,
        name="score",
    )(tokens, received.reshape(chips * query_len, dim_width))

    returned = lax.all_to_all(
        totals.reshape(chips, 1, pass_width), "blk", split_axis=0, concat_axis=0,
        axis_index_groups=same_core, tiled=True,
    ).reshape(chips, pass_width)
    spread = pl.pallas_call(
        turn_kernel,
        out_shape=jax.ShapeDtypeStruct((num_parts, CORES, part_width, chips), jnp.float32),
        in_specs=[VMEM],
        out_specs=VMEM,
        name="turn",
    )(returned)
    gathered = lax.all_to_all(
        spread.reshape(num_parts * CORES, part_width, chips), ("blk", "tok"), split_axis=0,
        concat_axis=0, axis_index_groups=around, tiled=True,
    ).reshape(num_parts, CORES, part_width, chips)

    named = turned.reshape(cand_count * query_count)
    order = jnp.arange(cand_count * query_count, dtype=jnp.int32)
    earlier = (named[:, None] == named[None, :]) & (order[:, None] < order[None, :])
    position = jnp.sum(earlier.astype(jnp.int32), axis=0)
    named_core = named % CORES
    lane = (named_core * chips + named // CORES).reshape(1, -1)
    plane = ((named_core ^ core) * 2 + position).reshape(1, -1)
    picked = pl.pallas_call(
        pick_kernel,
        out_shape=jax.ShapeDtypeStruct((cand_count, part_width, query_count), jnp.float32),
        in_specs=[VMEM, VMEM, VMEM],
        out_specs=VMEM,
        name="pick",
    )(gathered, lane, plane)
    return jnp.transpose(picked, (2, 0, 1))


def solution(mesh):
    same_core, around, swap = make_groups(mesh)
    in_specs = (P("blk", None, None), P("blk", None), P("blk", "tok", None, None), P("blk", None))
    out_specs = P("blk", None, "tok")

    def local(queries, candidates, passages, lengths):
        return shards(
            queries, candidates, passages, lengths, same_core=same_core, around=around, swap=swap
        )

    return jax.shard_map(local, mesh=mesh, in_specs=in_specs, out_specs=out_specs, check_vma=False)
```

```python
import functools
import itertools
import math

import jax
import jax.numpy as jnp
from jax import lax
from jax.experimental import pallas as pl
from jax.experimental.pallas import tpu as pltpu
from jax.sharding import PartitionSpec as P


CORES = 2
FLAG = 2.0
VMEM = pl.BlockSpec(memory_space=pltpu.VMEM)
SMEM = pl.BlockSpec(memory_space=pltpu.SMEM)
LANES = 128


def build_kernel(cand_ref, query_ref, out_ref, table, *, turn):
    pair_k, pair_q = cand_ref.shape
    owners = table.shape[0]
    core = lax.axis_index("blk") % CORES
    plane = lax.axis_index("tok")
    owner_core = core ^ (plane // 2)
    backward = plane % 2 == 0
    pairs = pair_k * pair_q
    for d in range(owners):
        table[d] = 0
    for i in range(pairs):
        p = jnp.where(backward, pairs - 1 - i, i)
        table[cand_ref[p // pair_q, p % pair_q]] = p % pair_q
    chips = owners // CORES
    for place in range(chips):
        chip = (place + turn) % chips
        out_ref[place] = query_ref[table[chip * CORES + owner_core]]


def score_kernel(*refs, tile, piece, query_len):
    *part_refs, query_ref, out_ref, token_ref = refs
    slots_len, width, dim = token_ref.shape
    length = part_refs[0].shape[0]
    items = tile // query_len
    plane = lax.axis_index("tok")
    first = part_refs[0][0]
    for shift in range(1, len(part_refs)):
        first = jnp.where(plane == shift, part_refs[shift][0], first)
    for shift, part_ref in enumerate(part_refs):
        for j in range(length):
            token = part_ref[j]
            token_ref[shift * length + j] = jnp.where(token > 1, first, token)

    def one_tile(index, carry):
        rows = query_ref[pl.ds(pl.multiple_of(index * tile, tile), tile), :]
        best = None
        for start in range(0, slots_len, piece):
            segment = token_ref[start : start + piece].reshape(piece * width, dim)
            scores = lax.dot_general(
                segment, rows, (((1,), (1,)), ((), ())), preferred_element_type=jnp.float32
            )
            top = jnp.max(scores.reshape(piece, width, tile), axis=0)
            best = top if best is None else jnp.maximum(best, top)
        flipped = jnp.transpose(best).reshape(items, query_len, width)
        out_ref[pl.ds(pl.multiple_of(index * items, items), items), :] = jnp.sum(flipped, axis=1)
        return carry

    lax.fori_loop(0, query_ref.shape[0] // tile, one_tile, 0)


def turn_kernel(in_ref, out_ref):
    parts, part_width, _ = out_ref.shape
    slots = in_ref.shape[0]
    flipped = jnp.transpose(in_ref[...])
    flipped = jnp.concatenate([flipped] * (LANES // slots), axis=1)
    for part in range(parts):
        out_ref[part] = flipped[part * part_width : (part + 1) * part_width]


def pick_kernel(in_ref, lane_ref, plane_ref, out_ref):
    planes, part_width, _ = in_ref.shape
    cand_count, _, query_count = out_ref.shape
    lanes = jnp.broadcast_to(lane_ref[...], (part_width, LANES))
    which = jnp.broadcast_to(plane_ref[...], (part_width, LANES))
    picked = None
    for plane in range(planes):
        got = jnp.take_along_axis(in_ref[plane], lanes, axis=1)
        picked = got if picked is None else jnp.where(which == plane, got, picked)
    for k in range(cand_count):
        out_ref[k] = picked[:, k * query_count : (k + 1) * query_count]


def near(*arrays):
    return [pltpu.with_memory_space_constraint(array, pltpu.VMEM) for array in arrays]


def make_groups(mesh):
    owners = mesh.shape["blk"]
    parts = mesh.shape["tok"]
    chips = owners // CORES
    turn = chips // 2 + math.isqrt(chips) // 2
    across = [[(place + turn) % chips * CORES + core for place in range(chips)] for core in range(CORES)]
    routes = []
    for shift in range(parts):
        pairs = []
        for blk, part in itertools.product(range(owners), range(parts)):
            plane = (part + shift) % parts
            pairs.append((blk * parts + part, (blk ^ (plane // 2)) * parts + plane))
        routes.append(pairs)
    return dict(across=across, routes=routes, turn=turn)


def shards(queries, candidates, passages, lengths, *, across, routes, turn):
    num_owners = lax.axis_size("blk")
    num_parts = lax.axis_size("tok")
    part_idx = lax.axis_index("tok")
    core = lax.axis_index("blk") % CORES
    query_count, query_len, dim_width = queries.shape
    cand_count = candidates.shape[1]
    local_len = passages.shape[1]
    pass_width = passages.shape[2]
    part_width = pass_width // num_parts
    chips = num_owners // CORES

    turned = candidates.T
    outgoing = pl.pallas_call(
        functools.partial(build_kernel, turn=turn),
        out_shape=pltpu.VMEM((chips, query_len, dim_width), queries.dtype),
        in_specs=[SMEM, VMEM],
        out_specs=VMEM,
        scratch_shapes=[pltpu.SMEM((num_owners,), jnp.int32)],
        name="build",
    )(turned, queries)
    received = lax.all_to_all(
        outgoing, "blk", split_axis=0, concat_axis=0, axis_index_groups=across, tiled=True
    )

    token_pos = part_idx * local_len + jnp.arange(local_len, dtype=jnp.int32)
    valid = token_pos[:, None] < lengths[0][None, :]
    flagged = jnp.where(valid[..., None], passages[0], jnp.array(FLAG, passages.dtype))
    parts = []
    for pairs in routes:
        parts.append(lax.ppermute(flagged, ("blk", "tok"), pairs))

    named = turned.reshape(cand_count * query_count)
    order = jnp.arange(cand_count * query_count, dtype=jnp.int32)
    earlier = (named[:, None] == named[None, :]) & (order[:, None] < order[None, :])
    position = jnp.sum(earlier.astype(jnp.int32), axis=0)
    lane = ((named // CORES - turn) % chips).reshape(1, -1)
    plane = (((named % CORES) ^ core) * 2 + position).reshape(1, -1)
    received, lane, plane = lax.optimization_barrier((received, lane, plane))
    totals = pl.pallas_call(
        lambda *refs: score_kernel(*refs, tile=512, piece=60, query_len=query_len),
        out_shape=pltpu.VMEM((chips, pass_width), jnp.float32),
        in_specs=[VMEM] * (num_parts + 1),
        out_specs=VMEM,
        scratch_shapes=[pltpu.VMEM((num_parts * local_len, pass_width, dim_width), passages.dtype)],
        name="score",
    )(*near(*parts, received.reshape(chips * query_len, dim_width)))

    returned = lax.all_to_all(
        totals.reshape(chips, 1, pass_width), "blk", split_axis=0, concat_axis=0,
        axis_index_groups=across, tiled=True,
    ).reshape(chips, pass_width)
    spread = pl.pallas_call(
        turn_kernel,
        out_shape=pltpu.VMEM((num_parts, part_width, LANES), jnp.float32),
        in_specs=[VMEM],
        out_specs=VMEM,
        name="turn",
    )(*near(returned))
    gathered = lax.all_to_all(spread, "tok", split_axis=0, concat_axis=0, tiled=True)

    picked = pl.pallas_call(
        pick_kernel,
        out_shape=jax.ShapeDtypeStruct((cand_count, part_width, query_count), jnp.float32),
        in_specs=[VMEM, VMEM, VMEM],
        out_specs=VMEM,
        name="pick",
    )(*near(gathered, lane, plane))
    return jnp.transpose(picked, (2, 0, 1))


def solution(mesh):
    in_specs = (P("blk", None, None), P("blk", None), P("blk", "tok", None, None), P("blk", None))
    out_specs = P("blk", None, "tok")
    groups = make_groups(mesh)

    def local(*args):
        return shards(*args, **groups)

    return jax.shard_map(local, mesh=mesh, in_specs=in_specs, out_specs=out_specs, check_vma=False)
```

```python
import functools
import itertools
import math

import jax
import jax.numpy as jnp
from jax import lax
from jax.experimental import pallas as pl
from jax.experimental.pallas import tpu as pltpu
from jax.sharding import PartitionSpec as P


CORES = 2
VMEM = pl.BlockSpec(memory_space=pltpu.VMEM)
SMEM = pl.BlockSpec(memory_space=pltpu.SMEM)
LANES = 128
TILE = 512
FIRST, SECOND = (0, 2), (1, 3)
NEGATIVE_FILL = -1e30


def build_kernel(cand_ref, query_hbm, out_ref, table, query_ref, sem, *, turn):
    fetch = pltpu.make_async_copy(query_hbm, query_ref, sem)
    fetch.start()
    pair_k, pair_q = cand_ref.shape
    owners = table.shape[0]
    chips = owners // CORES
    plane = lax.axis_index("tok")
    owner_core = lax.axis_index("blk") % CORES ^ (plane // 2)
    pairs = [(k, q) for k in range(pair_k) for q in range(pair_q)]
    for chip in range(chips):
        table[chip * CORES + owner_core] = 0

    @pl.when(plane % 2 == 0)
    def _():
        for k, q in reversed(pairs):
            table[cand_ref[k, q]] = q

    @pl.when(plane % 2 == 1)
    def _():
        for k, q in pairs:
            table[cand_ref[k, q]] = q

    fetch.wait()
    for place in range(chips):
        chip = (place + turn) % chips
        out_ref[place] = query_ref[table[chip * CORES + owner_core]]


def best_kernel(*refs, shifts, parts, tile, query_len, last):
    *given_refs, ends_ref, query_ref, out_ref, token_ref = refs
    part_refs, before_refs = given_refs[: len(shifts)], given_refs[len(shifts) :]
    length, width, dim = token_ref.shape[1:]
    items = tile // query_len
    plane = lax.axis_index("tok")
    ends = ends_ref[0].astype(jnp.float32)
    used = []
    for place, shift in enumerate(shifts):
        start = ((plane - shift + parts) % parts * length).astype(jnp.float32)
        used.append(jnp.concatenate([ends > start] * (tile // LANES), axis=1))
        left = (ends - start).astype(token_ref.dtype)
        first = part_refs[place][0]
        for j in range(length):
            token_ref[place, j] = jnp.where(left > j, part_refs[place][j], first)

    def one_tile(index, carry):
        rows = query_ref[pl.ds(pl.multiple_of(index * tile, tile), tile), :]
        best = before_refs[0][index] if before_refs else None
        for place in range(len(shifts)):
            scores = lax.dot_general(
                token_ref[place].reshape(length * width, dim), rows, (((1,), (1,)), ((), ())),
                preferred_element_type=jnp.float32,
            )
            top = jnp.max(scores.reshape(length, width, tile), axis=0)
            top = jnp.where(used[place], top, NEGATIVE_FILL)
            best = top if best is None else jnp.maximum(best, top)
        if last:
            flipped = jnp.transpose(best).reshape(items, query_len, width)
            out_ref[pl.ds(pl.multiple_of(index * items, items), items), :] = jnp.sum(flipped, axis=1)
        else:
            out_ref[index] = best
        return carry

    lax.fori_loop(0, query_ref.shape[0] // tile, one_tile, 0)


def turn_kernel(in_ref, out_ref):
    parts, part_width, _ = out_ref.shape
    slots = in_ref.shape[0]
    flipped = jnp.transpose(in_ref[...])
    flipped = jnp.concatenate([flipped] * (LANES // slots), axis=1)
    for part in range(parts):
        out_ref[part] = flipped[part * part_width : (part + 1) * part_width]


def pick_kernel(in_ref, lane_ref, plane_ref, out_ref):
    planes, part_width, _ = in_ref.shape
    cand_count, _, query_count = out_ref.shape
    lanes = jnp.broadcast_to(lane_ref[...], (part_width, LANES))
    which = jnp.broadcast_to(plane_ref[...], (part_width, LANES))
    picked = None
    for plane in range(planes):
        got = jnp.take_along_axis(in_ref[plane], lanes, axis=1)
        picked = got if picked is None else jnp.where(which == plane, got, picked)
    for k in range(cand_count):
        out_ref[k] = picked[:, k * query_count : (k + 1) * query_count]


def near(*arrays):
    return [pltpu.with_memory_space_constraint(array, pltpu.VMEM) for array in arrays]


def make_groups(mesh):
    owners = mesh.shape["blk"]
    parts = mesh.shape["tok"]
    chips = owners // CORES
    turn = chips // 2 + math.isqrt(chips) // 2
    across = [[(place + turn) % chips * CORES + core for place in range(chips)] for core in range(CORES)]
    routes = []
    for shift in range(parts):
        pairs = []
        for blk, part in itertools.product(range(owners), range(parts)):
            plane = (part + shift) % parts
            pairs.append((blk * parts + part, (blk ^ (plane // 2)) * parts + plane))
        routes.append(pairs)
    return dict(across=across, routes=routes, turn=turn)


def shards(queries, candidates, passages, lengths, *, across, routes, turn):
    num_owners = lax.axis_size("blk")
    num_parts = lax.axis_size("tok")
    core = lax.axis_index("blk") % CORES
    query_count, query_len, dim_width = queries.shape
    cand_count = candidates.shape[1]
    local_len = passages.shape[1]
    pass_width = passages.shape[2]
    part_width = pass_width // num_parts
    chips = num_owners // CORES

    turned = candidates.T
    build = pl.pallas_call(
        functools.partial(build_kernel, turn=turn),
        out_shape=pltpu.VMEM((chips, query_len, dim_width), queries.dtype),
        in_specs=[SMEM, pl.BlockSpec(memory_space=pl.ANY)],
        out_specs=VMEM,
        scratch_shapes=[
            pltpu.SMEM((num_owners,), jnp.int32),
            pltpu.VMEM(queries.shape, queries.dtype),
            pltpu.SemaphoreType.DMA,
        ],
        name="build",
    )
    outgoing = build(turned, queries)
    received = lax.all_to_all(
        outgoing, "blk", split_axis=0, concat_axis=0, axis_index_groups=across, tiled=True
    )

    own = passages[0]
    ends = jnp.broadcast_to(lengths[0][None, :, None], (1, pass_width, dim_width)).astype(own.dtype)
    parts = []
    for shift, pairs in enumerate(routes):
        payload = own if shift else jnp.concatenate([own, ends])
        parts.append(lax.ppermute(payload, ("blk", "tok"), pairs))

    named = turned.reshape(cand_count * query_count)
    order = jnp.arange(cand_count * query_count, dtype=jnp.int32)
    earlier = (named[:, None] == named[None, :]) & (order[:, None] < order[None, :])
    position = jnp.sum(earlier.astype(jnp.int32), axis=0)
    lane = ((named // CORES - turn) % chips).reshape(1, -1)
    plane = (((named % CORES) ^ core) * 2 + position).reshape(1, -1)
    received, lane, plane = lax.optimization_barrier((received, lane, plane))
    rows = received.reshape(chips * query_len, dim_width)
    ends = parts[0][local_len:]
    maxima = None
    for shifts in FIRST, SECOND:
        last = shifts is SECOND
        whole = (chips, pass_width) if last else (rows.shape[0] // TILE, pass_width, TILE)
        kernel = functools.partial(
            best_kernel, shifts=shifts, parts=num_parts, tile=TILE, query_len=query_len, last=last
        )
        inputs = [parts[shift] for shift in shifts] + ([maxima] if last else []) + [ends, rows]
        maxima = pl.pallas_call(
            kernel,
            out_shape=pltpu.VMEM(whole, jnp.float32),
            in_specs=[VMEM] * len(inputs),
            out_specs=VMEM,
            scratch_shapes=[pltpu.VMEM((len(shifts), local_len, pass_width, dim_width), own.dtype)],
            name="best",
        )(*near(*inputs))
    totals = maxima

    returned = lax.all_to_all(
        totals.reshape(chips, 1, pass_width), "blk", split_axis=0, concat_axis=0,
        axis_index_groups=across, tiled=True,
    ).reshape(chips, pass_width)
    spread = pl.pallas_call(
        turn_kernel,
        out_shape=pltpu.VMEM((num_parts, part_width, LANES), jnp.float32),
        in_specs=[VMEM],
        out_specs=VMEM,
        name="turn",
    )(*near(returned))
    gathered = lax.all_to_all(spread, "tok", split_axis=0, concat_axis=0, tiled=True)

    picked = pl.pallas_call(
        pick_kernel,
        out_shape=jax.ShapeDtypeStruct((cand_count, part_width, query_count), jnp.float32),
        in_specs=[VMEM, VMEM, VMEM],
        out_specs=VMEM,
        name="pick",
    )(*near(gathered, lane, plane))
    return jnp.transpose(picked, (2, 0, 1))


def solution(mesh):
    in_specs = (P("blk", None, None), P("blk", None), P("blk", "tok", None, None), P("blk", None))
    out_specs = P("blk", None, "tok")
    groups = make_groups(mesh)

    def local(*args):
        return shards(*args, **groups)

    return jax.shard_map(local, mesh=mesh, in_specs=in_specs, out_specs=out_specs, check_vma=False)
```

```python
import functools
import itertools
import math

import jax
import jax.numpy as jnp
from jax import lax
from jax.experimental import pallas as pl
from jax.experimental.pallas import tpu as pltpu
from jax.sharding import PartitionSpec as P


CORES = 2
VMEM = pl.BlockSpec(memory_space=pltpu.VMEM)
SMEM = pl.BlockSpec(memory_space=pltpu.SMEM)
LANES = 128
TILE = 512
FIRST, SECOND = (0, 2), (1, 3)
NEGATIVE_FILL = -1e30


def build_kernel(cand_hbm, query_hbm, out_ref, table, cand_ref, query_ref, sems, *, turn):
    named = pltpu.make_async_copy(cand_hbm, cand_ref, sems.at[0])
    fetch = pltpu.make_async_copy(query_hbm, query_ref, sems.at[1])
    named.start()
    fetch.start()
    pair_k, pair_q = cand_ref.shape
    owners = table.shape[0]
    chips = owners // CORES
    plane = lax.axis_index("tok")
    owner_core = lax.axis_index("blk") % CORES ^ (plane // 2)
    pairs = [(k, q) for k in range(pair_k) for q in range(pair_q)]
    for chip in range(chips):
        table[chip * CORES + owner_core] = 0
    named.wait()

    @pl.when(plane % 2 == 0)
    def _():
        for k, q in reversed(pairs):
            table[cand_ref[k, q]] = q

    @pl.when(plane % 2 == 1)
    def _():
        for k, q in pairs:
            table[cand_ref[k, q]] = q

    fetch.wait()
    for place in range(chips):
        chip = (place + turn) % chips
        out_ref[place] = query_ref[table[chip * CORES + owner_core]]


def best_kernel(*refs, shifts, parts, tile, query_len, delta, last):
    *given_refs, ends_ref, query_ref, out_ref, token_ref = refs
    part_refs, before_refs = given_refs[: len(shifts)], given_refs[len(shifts) :]
    length, width, dim = token_ref.shape[1:]
    items = tile // query_len
    plane = lax.axis_index("tok")
    ends = ends_ref[0].astype(jnp.float32)
    used = []
    for place, shift in enumerate(shifts):
        start = ((plane - shift + parts) % parts * length).astype(jnp.float32)
        used.append(jnp.concatenate([ends > start] * (tile // LANES), axis=1))
        left = (ends - start).astype(token_ref.dtype)
        first = part_refs[place][0]
        for j in range(length):
            token_ref[place, j] = jnp.where(left > j, part_refs[place][j], first)

    def one_tile(index, carry):
        rows = query_ref[pl.ds(pl.multiple_of(index * tile, tile), tile), :]
        best = before_refs[0][index] if before_refs else None
        for place in range(len(shifts)):
            scores = lax.dot_general(
                token_ref[place].reshape(length * width, dim), rows, (((1,), (1,)), ((), ())),
                preferred_element_type=jnp.float32,
            )
            top = jnp.max(scores.reshape(length, width, tile), axis=0)
            top = jnp.where(used[place], top, NEGATIVE_FILL)
            best = top if best is None else jnp.maximum(best, top)
        if last:
            flipped = jnp.transpose(best).reshape(items, query_len, width)
            row = (index * items + delta) % out_ref.shape[0]
            out_ref[pl.ds(pl.multiple_of(row, items), items), :] = jnp.sum(flipped, axis=1)
        else:
            out_ref[index] = best
        return carry

    lax.fori_loop(0, query_ref.shape[0] // tile, one_tile, 0)


def turn_kernel(in_ref, out_ref):
    parts, part_width, _ = out_ref.shape
    slots = in_ref.shape[0]
    flipped = jnp.transpose(in_ref[...])
    flipped = jnp.concatenate([flipped] * (LANES // slots), axis=1)
    for part in range(parts):
        out_ref[part] = flipped[part * part_width : (part + 1) * part_width]


def pick_kernel(in_ref, lane_ref, plane_ref, out_ref):
    planes, part_width, _ = in_ref.shape
    cand_count, _, query_count = out_ref.shape
    lanes = jnp.broadcast_to(lane_ref[...], (part_width, LANES))
    which = jnp.broadcast_to(plane_ref[...], (part_width, LANES))
    picked = None
    for plane in range(planes):
        got = jnp.take_along_axis(in_ref[plane], lanes, axis=1)
        picked = got if picked is None else jnp.where(which == plane, got, picked)
    for k in range(cand_count):
        out_ref[k] = picked[:, k * query_count : (k + 1) * query_count]


def near(*arrays):
    return [pltpu.with_memory_space_constraint(array, pltpu.VMEM) for array in arrays]


def make_groups(mesh):
    owners = mesh.shape["blk"]
    parts = mesh.shape["tok"]
    chips = owners // CORES
    turn = chips // 2 + chips // 8 + math.isqrt(chips) // 2
    back = turn

    def same_core(start):
        return [[(place + start) % chips * CORES + core for place in range(chips)] for core in range(CORES)]

    routes = []
    for shift in range(parts):
        pairs = []
        for blk, part in itertools.product(range(owners), range(parts)):
            plane = (part + shift) % parts
            pairs.append((blk * parts + part, (blk ^ (plane // 2)) * parts + plane))
        routes.append(pairs)
    return dict(across=same_core(turn), homeward=same_core(back), routes=routes, turn=turn, back=back)


def shards(queries, candidates, passages, lengths, *, across, homeward, routes, turn, back):
    num_owners = lax.axis_size("blk")
    num_parts = lax.axis_size("tok")
    core = lax.axis_index("blk") % CORES
    query_count, query_len, dim_width = queries.shape
    cand_count = candidates.shape[1]
    local_len = passages.shape[1]
    pass_width = passages.shape[2]
    part_width = pass_width // num_parts
    chips = num_owners // CORES

    turned = candidates.T
    build = pl.pallas_call(
        functools.partial(build_kernel, turn=turn),
        out_shape=pltpu.VMEM((chips, query_len, dim_width), queries.dtype),
        in_specs=[pl.BlockSpec(memory_space=pl.ANY)] * 2,
        out_specs=VMEM,
        scratch_shapes=[
            pltpu.SMEM((num_owners,), jnp.int32),
            pltpu.SMEM(turned.shape, turned.dtype),
            pltpu.VMEM(queries.shape, queries.dtype),
            pltpu.SemaphoreType.DMA((2,)),
        ],
        name="build",
    )
    outgoing = build(turned, queries)
    received = lax.all_to_all(
        outgoing, "blk", split_axis=0, concat_axis=0, axis_index_groups=across, tiled=True
    )

    own = passages[0]
    ends = jnp.broadcast_to(lengths[0][None, :, None], (1, pass_width, dim_width)).astype(own.dtype)
    parts = []
    for shift, pairs in enumerate(routes):
        payload = own if shift else jnp.concatenate([own, ends])
        parts.append(lax.ppermute(payload, ("blk", "tok"), pairs))

    named = turned.reshape(cand_count * query_count)
    order = jnp.arange(cand_count * query_count, dtype=jnp.int32)
    earlier = (named[:, None] == named[None, :]) & (order[:, None] < order[None, :])
    position = jnp.sum(earlier.astype(jnp.int32), axis=0)
    lane = ((named // CORES - back) % chips).reshape(1, -1)
    plane = (((named % CORES) ^ core) * 2 + position).reshape(1, -1)
    received, lane, plane = lax.optimization_barrier((received, lane, plane))
    rows = received.reshape(chips * query_len, dim_width)
    ends = parts[0][local_len:]
    maxima = None
    for shifts in FIRST, SECOND:
        last = shifts is SECOND
        whole = (chips, pass_width) if last else (rows.shape[0] // TILE, pass_width, TILE)
        kernel = functools.partial(
            best_kernel, shifts=shifts, parts=num_parts, tile=TILE, query_len=query_len,
            delta=(turn - back) % chips, last=last
        )
        inputs = [parts[shift] for shift in shifts] + ([maxima] if last else []) + [ends, rows]
        maxima = pl.pallas_call(
            kernel,
            out_shape=pltpu.VMEM(whole, jnp.float32),
            in_specs=[VMEM] * len(inputs),
            out_specs=VMEM,
            scratch_shapes=[pltpu.VMEM((len(shifts), local_len, pass_width, dim_width), own.dtype)],
            name="best",
        )(*near(*inputs))
    totals = maxima

    returned = lax.all_to_all(
        totals.reshape(chips, 1, pass_width), "blk", split_axis=0, concat_axis=0,
        axis_index_groups=homeward, tiled=True,
    ).reshape(chips, pass_width)
    spread = pl.pallas_call(
        turn_kernel,
        out_shape=pltpu.VMEM((num_parts, part_width, LANES), jnp.float32),
        in_specs=[VMEM],
        out_specs=VMEM,
        name="turn",
    )(*near(returned))
    gathered = lax.all_to_all(spread, "tok", split_axis=0, concat_axis=0, tiled=True)

    picked = pl.pallas_call(
        pick_kernel,
        out_shape=jax.ShapeDtypeStruct((cand_count, part_width, query_count), jnp.float32),
        in_specs=[VMEM, VMEM, VMEM],
        out_specs=VMEM,
        name="pick",
    )(*near(gathered, lane, plane))
    return jnp.transpose(picked, (2, 0, 1))


def solution(mesh):
    in_specs = (P("blk", None, None), P("blk", None), P("blk", "tok", None, None), P("blk", None))
    out_specs = P("blk", None, "tok")
    groups = make_groups(mesh)

    def local(*args):
        return shards(*args, **groups)

    return jax.shard_map(local, mesh=mesh, in_specs=in_specs, out_specs=out_specs, check_vma=False)
```

```python
import functools
import itertools
import math

import jax
import jax.numpy as jnp
from jax import lax
from jax.experimental import pallas as pl
from jax.experimental.pallas import tpu as pltpu
from jax.sharding import PartitionSpec as P


CORES = 2
VMEM = pl.BlockSpec(memory_space=pltpu.VMEM)
SMEM = pl.BlockSpec(memory_space=pltpu.SMEM)
LANES = 128
TILE = 2048
FIRST, SECOND = (0, 2), (1, 3)
NEGATIVE_FILL = -1e30


def build_kernel(cand_hbm, query_hbm, out_ref, table, cand_ref, query_ref, sems, *, turn):
    named = pltpu.make_async_copy(cand_hbm, cand_ref, sems.at[0])
    fetch = pltpu.make_async_copy(query_hbm, query_ref, sems.at[1])
    named.start()
    fetch.start()
    pair_k, pair_q = cand_ref.shape
    owners = table.shape[0]
    chips = owners // CORES
    plane = lax.axis_index("tok")
    owner_core = lax.axis_index("blk") % CORES ^ (plane // 2)
    pairs = [(k, q) for k in range(pair_k) for q in range(pair_q)]
    for chip in range(chips):
        table[chip * CORES + owner_core] = 0
    named.wait()

    @pl.when(plane % 2 == 0)
    def _():
        for k, q in reversed(pairs):
            table[cand_ref[k, q]] = q

    @pl.when(plane % 2 == 1)
    def _():
        for k, q in pairs:
            table[cand_ref[k, q]] = q

    fetch.wait()
    for place in range(chips):
        chip = (place + turn) % chips
        out_ref[place] = query_ref[table[chip * CORES + owner_core]]


def best_kernel(*refs, shifts, parts, tile, query_len, last):
    *given_refs, ends_ref, query_ref, out_ref, token_ref = refs
    part_refs, before_refs = given_refs[: len(shifts)], given_refs[len(shifts) :]
    length, width, dim = token_ref.shape[1:]
    items = tile // query_len
    plane = lax.axis_index("tok")
    ends = ends_ref[0].astype(jnp.float32)
    used = []
    for place, shift in enumerate(shifts):
        start = ((plane - shift + parts) % parts * length).astype(jnp.float32)
        used.append(jnp.concatenate([ends > start] * (tile // LANES), axis=1))
        left = (ends - start).astype(token_ref.dtype)
        first = part_refs[place][0]
        for j in range(length):
            token_ref[place, j] = jnp.where(left > j, part_refs[place][j], first)

    def one_tile(index, carry):
        rows = query_ref[pl.ds(pl.multiple_of(index * tile, tile), tile), :]
        best = before_refs[0][index] if before_refs else None
        for place in range(len(shifts)):
            scores = lax.dot_general(
                token_ref[place].reshape(length * width, dim), rows, (((1,), (1,)), ((), ())),
                preferred_element_type=jnp.float32,
            )
            top = jnp.max(scores.reshape(length, width, tile), axis=0)
            top = jnp.where(used[place], top, NEGATIVE_FILL)
            best = top if best is None else jnp.maximum(best, top)
        if last:
            flipped = jnp.transpose(best).reshape(items, query_len, width)
            out_ref[pl.ds(pl.multiple_of(index * items, items), items), :] = jnp.sum(flipped, axis=1)
        else:
            out_ref[index] = best
        return carry

    lax.fori_loop(0, query_ref.shape[0] // tile, one_tile, 0)


def turn_kernel(in_ref, out_ref):
    parts, part_width, _ = out_ref.shape
    slots = in_ref.shape[0]
    flipped = jnp.transpose(in_ref[...])
    flipped = jnp.concatenate([flipped] * (LANES // slots), axis=1)
    for part in range(parts):
        out_ref[part] = flipped[part * part_width : (part + 1) * part_width]


def pick_kernel(in_ref, lane_ref, plane_ref, out_ref):
    planes, part_width, _ = in_ref.shape
    cand_count, _, query_count = out_ref.shape
    lanes = jnp.broadcast_to(lane_ref[...], (part_width, LANES))
    which = jnp.broadcast_to(plane_ref[...], (part_width, LANES))
    picked = None
    for plane in range(planes):
        got = jnp.take_along_axis(in_ref[plane], lanes, axis=1)
        picked = got if picked is None else jnp.where(which == plane, got, picked)
    for k in range(cand_count):
        out_ref[k] = picked[:, k * query_count : (k + 1) * query_count]


def near(*arrays):
    return [pltpu.with_memory_space_constraint(array, pltpu.VMEM) for array in arrays]


def make_groups(mesh):
    owners = mesh.shape["blk"]
    parts = mesh.shape["tok"]
    chips = owners // CORES
    turn = chips // 2 + chips // 8 + math.isqrt(chips) // 2
    across = [[(place + turn) % chips * CORES + core for place in range(chips)] for core in range(CORES)]
    routes = []
    for shift in range(parts):
        pairs = []
        for blk, part in itertools.product(range(owners), range(parts)):
            plane = (part + shift) % parts
            pairs.append((blk * parts + part, (blk ^ (plane // 2)) * parts + plane))
        routes.append(pairs)
    return dict(across=across, routes=routes, turn=turn)


def shards(queries, candidates, passages, lengths, *, across, routes, turn):
    num_owners = lax.axis_size("blk")
    num_parts = lax.axis_size("tok")
    core = lax.axis_index("blk") % CORES
    query_count, query_len, dim_width = queries.shape
    cand_count = candidates.shape[1]
    local_len = passages.shape[1]
    pass_width = passages.shape[2]
    part_width = pass_width // num_parts
    chips = num_owners // CORES

    turned = candidates.T
    build = pl.pallas_call(
        functools.partial(build_kernel, turn=turn),
        out_shape=pltpu.VMEM((chips, query_len, dim_width), queries.dtype),
        in_specs=[pl.BlockSpec(memory_space=pl.ANY)] * 2,
        out_specs=VMEM,
        scratch_shapes=[
            pltpu.SMEM((num_owners,), jnp.int32),
            pltpu.SMEM(turned.shape, turned.dtype),
            pltpu.VMEM(queries.shape, queries.dtype),
            pltpu.SemaphoreType.DMA((2,)),
        ],
        name="build",
    )
    outgoing = build(turned, queries)
    received = lax.all_to_all(
        outgoing, "blk", split_axis=0, concat_axis=0, axis_index_groups=across, tiled=True
    )

    own = passages[0]
    ends = jnp.broadcast_to(lengths[0][None, :, None], (1, pass_width, dim_width)).astype(own.dtype)
    parts = []
    for shift, pairs in enumerate(routes):
        payload = own if shift else jnp.concatenate([own, ends])
        parts.append(lax.ppermute(payload, ("blk", "tok"), pairs))

    named = turned.reshape(cand_count * query_count)
    order = jnp.arange(cand_count * query_count, dtype=jnp.int32)
    earlier = (named[:, None] == named[None, :]) & (order[:, None] < order[None, :])
    position = jnp.sum(earlier.astype(jnp.int32), axis=0)
    lane = ((named // CORES - turn) % chips).reshape(1, -1)
    plane = (((named % CORES) ^ core) * 2 + position).reshape(1, -1)
    received, lane, plane = lax.optimization_barrier((received, lane, plane))
    rows = received.reshape(chips * query_len, dim_width)
    ends = parts[0][local_len:]
    maxima = None
    for shifts in FIRST, SECOND:
        last = shifts is SECOND
        whole = (chips, pass_width) if last else (rows.shape[0] // TILE, pass_width, TILE)
        kernel = functools.partial(
            best_kernel, shifts=shifts, parts=num_parts, tile=TILE, query_len=query_len, last=last
        )
        inputs = [parts[shift] for shift in shifts] + ([maxima] if last else []) + [ends, rows]
        maxima = pl.pallas_call(
            kernel,
            out_shape=pltpu.VMEM(whole, jnp.float32),
            in_specs=[VMEM] * len(inputs),
            out_specs=VMEM,
            scratch_shapes=[pltpu.VMEM((len(shifts), local_len, pass_width, dim_width), own.dtype)],
            name="best",
        )(*near(*inputs))
    totals = maxima

    returned = lax.all_to_all(
        totals.reshape(chips, 1, pass_width), "blk", split_axis=0, concat_axis=0,
        axis_index_groups=across, tiled=True,
    ).reshape(chips, pass_width)
    spread = pl.pallas_call(
        turn_kernel,
        out_shape=pltpu.VMEM((num_parts, part_width, LANES), jnp.float32),
        in_specs=[VMEM],
        out_specs=VMEM,
        name="turn",
    )(*near(returned))
    gathered = lax.all_to_all(spread, "tok", split_axis=0, concat_axis=0, tiled=True)

    picked = pl.pallas_call(
        pick_kernel,
        out_shape=jax.ShapeDtypeStruct((cand_count, part_width, query_count), jnp.float32),
        in_specs=[VMEM, VMEM, VMEM],
        out_specs=VMEM,
        name="pick",
    )(*near(gathered, lane, plane))
    return jnp.transpose(picked, (2, 0, 1))


def solution(mesh):
    in_specs = (P("blk", None, None), P("blk", None), P("blk", "tok", None, None), P("blk", None))
    out_specs = P("blk", None, "tok")
    groups = make_groups(mesh)

    def local(*args):
        return shards(*args, **groups)

    return jax.shard_map(local, mesh=mesh, in_specs=in_specs, out_specs=out_specs, check_vma=False)
```

```python
import functools
import itertools
import math

import jax
import jax.numpy as jnp
from jax import lax
from jax.experimental import pallas as pl
from jax.experimental.pallas import tpu as pltpu
from jax.sharding import PartitionSpec as P


CORES = 2
VMEM = pl.BlockSpec(memory_space=pltpu.VMEM)
SMEM = pl.BlockSpec(memory_space=pltpu.SMEM)
LANES = 128
TILE = 2048
FIRST, SECOND = (0, 2), (1, 3)
NEGATIVE_FILL = -1e30


def build_kernel(cand_hbm, query_hbm, out_ref, table, cand_ref, query_ref, sems, *, turn):
    named = pltpu.make_async_copy(cand_hbm, cand_ref, sems.at[0])
    fetch = pltpu.make_async_copy(query_hbm, query_ref, sems.at[1])
    named.start()
    fetch.start()
    pair_k, pair_q = cand_ref.shape
    owners = table.shape[0]
    chips = owners // CORES
    plane = lax.axis_index("tok")
    owner_core = lax.axis_index("blk") % CORES ^ (plane // 2)
    pairs = [(k, q) for k in range(pair_k) for q in range(pair_q)]
    for chip in range(chips):
        table[chip * CORES + owner_core] = 0
    named.wait()

    @pl.when(plane % 2 == 0)
    def _():
        for k, q in reversed(pairs):
            table[cand_ref[k, q]] = q

    @pl.when(plane % 2 == 1)
    def _():
        for k, q in pairs:
            table[cand_ref[k, q]] = q

    fetch.wait()
    for place in range(chips):
        chip = (place + turn) % chips
        out_ref[place] = query_ref[table[chip * CORES + owner_core]]


def fill_slices(part_refs, ends_ref, token_ref, shifts, parts):
    length = token_ref.shape[1]
    ends = ends_ref[0].astype(jnp.float32)
    plane = lax.axis_index("tok")
    for place, shift in enumerate(shifts):
        start = ((plane - shift + parts) % parts * length).astype(jnp.float32)
        left = (ends - start).astype(token_ref.dtype)
        first = part_refs[place][0]
        for j in range(length):
            token_ref[place, j] = jnp.where(left > j, part_refs[place][j], first)


def fill_kernel(*refs, shifts, parts):
    *part_refs, ends_ref, token_ref = refs
    fill_slices(part_refs, ends_ref, token_ref, shifts, parts)


def best_kernel(*refs, shifts, parts, tile, query_len, last):
    if last:
        *part_refs, before_ref, ends_ref, query_ref, out_ref, token_ref = refs
        before_refs = [before_ref]
        fill_slices(part_refs, ends_ref, token_ref, shifts, parts)
    else:
        token_ref, ends_ref, query_ref, out_ref = refs
        before_refs = []
    length, width, dim = token_ref.shape[1:]
    items = tile // query_len
    plane = lax.axis_index("tok")
    ends = ends_ref[0].astype(jnp.float32)
    used = []
    for shift in shifts:
        start = ((plane - shift + parts) % parts * length).astype(jnp.float32)
        used.append(jnp.concatenate([ends > start] * (tile // LANES), axis=1))

    def one_tile(index, carry):
        rows = query_ref[pl.ds(pl.multiple_of(index * tile, tile), tile), :]
        best = before_refs[0][index] if before_refs else None
        for place in range(len(shifts)):
            scores = lax.dot_general(
                token_ref[place].reshape(length * width, dim), rows, (((1,), (1,)), ((), ())),
                preferred_element_type=jnp.float32,
            )
            top = jnp.max(scores.reshape(length, width, tile), axis=0)
            top = jnp.where(used[place], top, NEGATIVE_FILL)
            best = top if best is None else jnp.maximum(best, top)
        if last:
            flipped = jnp.transpose(best).reshape(items, query_len, width)
            out_ref[pl.ds(pl.multiple_of(index * items, items), items), :] = jnp.sum(flipped, axis=1)
        else:
            out_ref[index] = best
        return carry

    lax.fori_loop(0, query_ref.shape[0] // tile, one_tile, 0)


def turn_kernel(in_ref, out_ref):
    parts, part_width, _ = out_ref.shape
    slots = in_ref.shape[0]
    flipped = jnp.transpose(in_ref[...])
    flipped = jnp.concatenate([flipped] * (LANES // slots), axis=1)
    for part in range(parts):
        out_ref[part] = flipped[part * part_width : (part + 1) * part_width]


def pick_kernel(in_ref, lane_ref, plane_ref, out_ref):
    planes, part_width, _ = in_ref.shape
    cand_count, _, query_count = out_ref.shape
    lanes = jnp.broadcast_to(lane_ref[...], (part_width, LANES))
    which = jnp.broadcast_to(plane_ref[...], (part_width, LANES))
    picked = None
    for plane in range(planes):
        got = jnp.take_along_axis(in_ref[plane], lanes, axis=1)
        picked = got if picked is None else jnp.where(which == plane, got, picked)
    for k in range(cand_count):
        out_ref[k] = picked[:, k * query_count : (k + 1) * query_count]


def near(*arrays):
    return [pltpu.with_memory_space_constraint(array, pltpu.VMEM) for array in arrays]


def make_groups(mesh):
    owners = mesh.shape["blk"]
    parts = mesh.shape["tok"]
    chips = owners // CORES
    turn = chips // 2 + chips // 8 + math.isqrt(chips) // 2
    across = [[(place + turn) % chips * CORES + core for place in range(chips)] for core in range(CORES)]
    routes = []
    for shift in range(parts):
        pairs = []
        for blk, part in itertools.product(range(owners), range(parts)):
            plane = (part + shift) % parts
            pairs.append((blk * parts + part, (blk ^ (plane // 2)) * parts + plane))
        routes.append(pairs)
    return dict(across=across, routes=routes, turn=turn)


def shards(queries, candidates, passages, lengths, *, across, routes, turn):
    num_owners = lax.axis_size("blk")
    num_parts = lax.axis_size("tok")
    core = lax.axis_index("blk") % CORES
    query_count, query_len, dim_width = queries.shape
    cand_count = candidates.shape[1]
    local_len = passages.shape[1]
    pass_width = passages.shape[2]
    part_width = pass_width // num_parts
    chips = num_owners // CORES

    turned = candidates.T
    build = pl.pallas_call(
        functools.partial(build_kernel, turn=turn),
        out_shape=pltpu.VMEM((chips, query_len, dim_width), queries.dtype),
        in_specs=[pl.BlockSpec(memory_space=pl.ANY)] * 2,
        out_specs=VMEM,
        scratch_shapes=[
            pltpu.SMEM((num_owners,), jnp.int32),
            pltpu.SMEM(turned.shape, turned.dtype),
            pltpu.VMEM(queries.shape, queries.dtype),
            pltpu.SemaphoreType.DMA((2,)),
        ],
        name="build",
    )
    outgoing = build(turned, queries)
    received = lax.all_to_all(
        outgoing, "blk", split_axis=0, concat_axis=0, axis_index_groups=across, tiled=True
    )

    own = passages[0]
    ends = jnp.broadcast_to(lengths[0][None, :, None], (1, pass_width, dim_width)).astype(own.dtype)
    parts = []
    for shift, pairs in enumerate(routes):
        payload = own if shift else jnp.concatenate([own, ends])
        parts.append(lax.ppermute(payload, ("blk", "tok"), pairs))

    named = turned.reshape(cand_count * query_count)
    order = jnp.arange(cand_count * query_count, dtype=jnp.int32)
    earlier = (named[:, None] == named[None, :]) & (order[:, None] < order[None, :])
    position = jnp.sum(earlier.astype(jnp.int32), axis=0)
    lane = ((named // CORES - turn) % chips).reshape(1, -1)
    plane = (((named % CORES) ^ core) * 2 + position).reshape(1, -1)
    received, lane, plane = lax.optimization_barrier((received, lane, plane))
    rows = received.reshape(chips * query_len, dim_width)
    ends = parts[0][local_len:]
    maxima = None
    for shifts in FIRST, SECOND:
        last = shifts is SECOND
        whole = (chips, pass_width) if last else (rows.shape[0] // TILE, pass_width, TILE)
        kernel = functools.partial(
            best_kernel, shifts=shifts, parts=num_parts, tile=TILE, query_len=query_len, last=last
        )
        slices = [parts[shift] for shift in shifts]
        shape = (len(shifts), local_len, pass_width, dim_width)
        if last:
            inputs = slices + [maxima, ends, rows]
        else:
            filled = pl.pallas_call(
                functools.partial(fill_kernel, shifts=shifts, parts=num_parts),
                out_shape=pltpu.VMEM(shape, own.dtype),
                in_specs=[VMEM] * (len(slices) + 1),
                out_specs=VMEM,
                name="fill",
            )(*near(*slices, ends))
            inputs = [filled, ends, rows]
        maxima = pl.pallas_call(
            kernel,
            out_shape=pltpu.VMEM(whole, jnp.float32),
            in_specs=[VMEM] * len(inputs),
            out_specs=VMEM,
            scratch_shapes=[pltpu.VMEM(shape, own.dtype)] if last else [],
            name="best",
        )(*near(*inputs))
    totals = maxima

    returned = lax.all_to_all(
        totals.reshape(chips, 1, pass_width), "blk", split_axis=0, concat_axis=0,
        axis_index_groups=across, tiled=True,
    ).reshape(chips, pass_width)
    spread = pl.pallas_call(
        turn_kernel,
        out_shape=pltpu.VMEM((num_parts, part_width, LANES), jnp.float32),
        in_specs=[VMEM],
        out_specs=VMEM,
        name="turn",
    )(*near(returned))
    gathered = lax.all_to_all(spread, "tok", split_axis=0, concat_axis=0, tiled=True)

    picked = pl.pallas_call(
        pick_kernel,
        out_shape=jax.ShapeDtypeStruct((cand_count, part_width, query_count), jnp.float32),
        in_specs=[VMEM, VMEM, VMEM],
        out_specs=VMEM,
        name="pick",
    )(*near(gathered, lane, plane))
    return jnp.transpose(picked, (2, 0, 1))


def solution(mesh):
    in_specs = (P("blk", None, None), P("blk", None), P("blk", "tok", None, None), P("blk", None))
    out_specs = P("blk", None, "tok")
    groups = make_groups(mesh)

    def local(*args):
        return shards(*args, **groups)

    return jax.shard_map(local, mesh=mesh, in_specs=in_specs, out_specs=out_specs, check_vma=False)
```
